32 devices in a mesh: stream: 2 (over y), span: 4 (over z), wall: 4 (over x, core).
Axes of the slice: x: 2, y: 2, z: 4, core: 2. Of those that a mesh axis runs over, the one named last changes fastest.
Arguments:
- temp_in: float32 [8, 8, 8, 4096], P(None, None, None, ('stream', 'span', 'wall')), may hold values from -20 to 20
- velocity: bfloat16 [3, 8, 8, 8, 4096], P(None, None, None, None, ('stream', 'span', 'wall')), may hold values from -192 to 192
- spacing: float32 [3, 4096], P(None, ('stream', 'span', 'wall')), may hold values from 0.7 to 1.4
- conduct: float32 [4096], P(('stream', 'span', 'wall')), may hold values from 0.5 to 2
- shell_map: int32 [8, 8, 8, 32], P(None, None, 'stream', 'span'), may hold values from 0 to 4095, as said below
- shell_cond: float32 [16, 2048], P('stream', ('span', 'wall')), may hold values from 0.25 to 1
- shell_diag: float32 [16, 2048], P('stream', ('span', 'wall')), may hold values from 0.2 to 2
Outputs:
- temp_out: float32 [8, 8, 8, 4096], P(None, None, None, ('stream', 'span', 'wall'))
- shell_temp: float32 [16, 2048], P('stream', ('span', 'wall'))
- shell_resid: float32 [16, 2048], P('stream', ('span', 'wall'))
The draws below stay inside these ranges and needn't reach their ends.
Inputs may be any that keep to these rules, and one draw needn't show every extreme that they name: `shell_map`: among the wall points of one block of 4 x 8 wall faces that share a streamwise and a spanwise slab, at most 1024 name the same owner t // 1024, and exactly 1024 name one owner.
All inputs are finite; a program needn't handle non-finite values.
Results may differ from the reference program's by a relative error of at most 0.0003.
Values sent between devices are 32-bit elements; how exact they have to be, the bound alone decides.
A program may use at most 128 MiB of HBM per device.

```python
import math
import jax
import jax.numpy as jnp
import numpy as np
from jax import lax

EX = 4
EY = 8
EZ = 4
SX = 8
SY = 128
SUBSTEPS = 2
CG_ITERS = 2
ELEM_DEV = 128
ELEMS = 4096
STREAM_ELEMENTS = 8
SPAN_ELEMENTS = 32
WALL_ELEMENTS = 16
CAP = 1024
S_DEV = 1024
SXG = 16
SYG = 2048
N_STREAM = 2
N_SPAN = 4
N_WALL = 4


def draw_temp_in(key, part):
    element = jnp.arange(ELEMS)
    per_slab = ELEMS // N_STREAM
    stream_place = element // per_slab * EX + element % (EX * EY * EZ) // (EY * EZ)
    fraction = stream_place.astype(jnp.float32) / max(STREAM_ELEMENTS - 1, 1)
    rough_part = jnp.clip(jax.random.normal(key, (8, 8, 8, ELEMS), jnp.float32), -5.0, 5.0)
    envelope = 4.0 ** fraction
    return (rough_part * envelope[None, None, None, :]).astype(jnp.float32)


def draw_shell_map(key, part):
    point_count = 64 * EX * EY
    block_keys = jax.random.split(jax.random.fold_in(key, 17), N_STREAM * N_SPAN)

    def one_block(block_key):
        key_lead, key_rest, key_order, key_node = jax.random.split(block_key, 4)
        leader = jax.random.randint(key_lead, (), 0, N_WALL)
        others = (leader + 1 + jax.random.randint(key_rest, (point_count - CAP,), 0, N_WALL - 1)) % N_WALL
        owners = jnp.concatenate([jnp.full((CAP,), leader, jnp.int32), others.astype(jnp.int32)])
        owners = jax.random.permutation(key_order, owners)
        node_ids = jax.random.randint(key_node, (point_count,), 0, SX * SY)
        return (owners * (SX * SY) + node_ids).astype(jnp.int32)
    table = jax.vmap(one_block)(block_keys)
    table = table.reshape((N_STREAM, N_SPAN, 8, 8, EX, EY))
    table = table.transpose(2, 3, 0, 4, 1, 5)
    return table.reshape((8, 8, N_STREAM * EX, N_SPAN * EY))


def levels(own_key, dims, cuts, least, high):
    loudness = 1.0
    for dim, parts in cuts:
        steps = jax.random.uniform(jax.random.fold_in(jax.random.fold_in(own_key, 6), dim), (parts,), jnp.float32, least / len(cuts), high / len(cuts))
        loudness = loudness * jnp.repeat(jnp.exp(steps), dims[dim] // parts).reshape((-1,) + (1,) * (len(dims) - 1 - dim))
    return loudness


def noise(own_key, shape, width, limit, shards=(), dtype=jnp.bfloat16):
    drawn = jax.random.normal(own_key, shape, jnp.float32) * width
    if len(shards) > 0:
        drawn = levels(own_key, shape, shards, -0.22, 0.18) * drawn
    return jnp.clip(drawn, min=-limit, max=limit).astype(dtype)


def setup_inputs(seed: int = 0) -> dict:
    streams_of = jax.random.split(jax.random.key(seed), 8)
    return {
        "temp_in": draw_temp_in(jax.random.fold_in(streams_of[7], 71), 0),
        "velocity": noise(streams_of[1], (3, 8, 8, 8, ELEMS), 32.0, 192.0, ((4, 32),)),
        "spacing": jnp.clip(jnp.exp(math.log(1.4) - 0.6931472 * jax.random.uniform(streams_of[2], (3, ELEMS), jnp.float32) ** levels(streams_of[2], (3, ELEMS), ((1, 32),), -0.2, 0.2)), 0.7, 1.4),
        "conduct": jnp.clip(jnp.exp(math.log(2.0) - 1.3862944 * jax.random.uniform(streams_of[3], (ELEMS,), jnp.float32) ** levels(streams_of[3], (ELEMS,), ((0, 32),), -0.2, 0.2)), 0.5, 2.0),
        "shell_map": draw_shell_map(jax.random.fold_in(streams_of[7], 71), 0),
        "shell_cond": jnp.clip(jnp.exp(math.log(1.0) - 1.3862944 * jax.random.uniform(streams_of[5], (SXG, SYG), jnp.float32) ** levels(streams_of[5], (SXG, SYG), ((0, 2), (1, 16)), -0.2, 0.2)), 0.25, 1.0),
        "shell_diag": jnp.clip(jnp.exp(math.log(2.0) - 2.3025851 * jax.random.uniform(streams_of[6], (SXG, SYG), jnp.float32) ** levels(streams_of[6], (SXG, SYG), ((0, 2), (1, 16)), -0.2, 0.2)), 0.2, 2.0),
    }


time_step = 3.0e-5
highest = lax.Precision.HIGHEST


def gll_tables():
    degree = 7
    points = np.array([-1.0, -0.8717401485096066, -0.5917001814331423, -0.2092992179024789,
                       0.2092992179024789, 0.5917001814331423, 0.8717401485096066, 1.0])
    previous = np.ones(8)
    current = points.copy()
    for order in range(1, degree):
        following = ((2 * order + 1) * points * current - order * previous) / (order + 1)
        previous = current
        current = following
    values = current
    weights = 2.0 / (degree * (degree + 1) * values * values)
    differ = points[:, None] - points[None, :]
    safe_differ = np.where(differ == 0.0, 1.0, differ)
    matrix = np.where(differ == 0.0, 0.0, values[:, None] / (values[None, :] * safe_differ))
    matrix[0, 0] = -degree * (degree + 1) / 4.0
    matrix[degree, degree] = degree * (degree + 1) / 4.0
    return jnp.asarray(weights, jnp.float32), jnp.asarray(matrix, jnp.float32)


def element_mass(spacing, weights):
    cube_w = weights[:, None, None] * weights[None, :, None] * weights[None, None, :]
    volume = spacing[0] * spacing[1] * spacing[2] / 8.0
    return cube_w[:, :, :, None] * volume[None, None, None, :]


def element_rate(temp_field, velocity, spacing, conduct, point_mass, weights, matrix):
    scale_x = 2.0 / spacing[0]
    scale_y = 2.0 / spacing[1]
    scale_z = 2.0 / spacing[2]
    grad_x = jnp.einsum("ai,ijkn->ajkn", matrix, temp_field, precision=highest) * scale_x
    grad_y = jnp.einsum("bj,ijkn->ibkn", matrix, temp_field, precision=highest) * scale_y
    grad_z = jnp.einsum("ck,ijkn->ijcn", matrix, temp_field, precision=highest) * scale_z
    flow_vel = velocity.astype(jnp.float32)
    advect = flow_vel[0] * grad_x + flow_vel[1] * grad_y + flow_vel[2] * grad_z
    weighted = point_mass * conduct
    stiffness = scale_x * jnp.einsum("ai,ajkn->ijkn", matrix, weighted * grad_x, precision=highest)
    stiffness = stiffness + scale_y * jnp.einsum("bj,ibkn->ijkn", matrix, weighted * grad_y, precision=highest)
    stiffness = stiffness + scale_z * jnp.einsum("ck,ijcn->ijkn", matrix, weighted * grad_z, precision=highest)
    return -(point_mass * advect) - stiffness


def wall_flux(wall_field, wall_spacing, wall_conduct, weights, matrix):
    normal = jnp.einsum("k,ijkn->ijn", matrix[0], wall_field, precision=highest)
    face_area = weights[:, None, None] * weights[None, :, None] * (wall_spacing[0] * wall_spacing[1] / 4.0)[None, None, :]
    return wall_conduct * (2.0 / wall_spacing[2]) * normal * face_area


def to_grid(temp_field):
    reshaped_array = temp_field.reshape((8, 8, 8, N_STREAM, N_SPAN, N_WALL, EX, EY, EZ))
    return reshaped_array.transpose(0, 1, 2, 3, 6, 4, 7, 5, 8).reshape((8, 8, 8, STREAM_ELEMENTS, SPAN_ELEMENTS, WALL_ELEMENTS))


def from_grid(node_grid):
    reshaped_array = node_grid.reshape((8, 8, 8, N_STREAM, EX, N_SPAN, EY, N_WALL, EZ))
    return reshaped_array.transpose(0, 1, 2, 3, 5, 7, 4, 6, 8).reshape((8, 8, 8, ELEMS))


def pair_faces(node_grid, point_axis, place_axis, wraps_around):
    final_axis = node_grid.ndim - 1
    reordered = jnp.moveaxis(node_grid, (point_axis, place_axis), (0, final_axis))
    upper_face = reordered[7]
    lower_face = reordered[0]
    if wraps_around:
        shared = upper_face + jnp.roll(lower_face, -1, axis=-1)
        new_upper = shared
        new_lower = jnp.roll(shared, 1, axis=-1)
    else:
        shared = upper_face[..., :-1] + lower_face[..., 1:]
        new_upper = jnp.concatenate([shared, upper_face[..., -1:]], axis=-1)
        new_lower = jnp.concatenate([lower_face[..., :1], shared], axis=-1)
    reordered = reordered.at[7].set(new_upper).at[0].set(new_lower)
    return jnp.moveaxis(reordered, (0, final_axis), (point_axis, place_axis))


def direct_sum(temp_field):
    node_grid = to_grid(temp_field)
    node_grid = pair_faces(node_grid, 0, 3, False)
    node_grid = pair_faces(node_grid, 1, 4, True)
    node_grid = pair_faces(node_grid, 2, 5, False)
    return from_grid(node_grid)


def to_slabs(array):
    leading = array.shape[:-1]
    reshaped_array = array.reshape(leading + (N_STREAM, ELEMS // N_STREAM))
    return jnp.moveaxis(reshaped_array, -2, 0)


def from_slabs(array):
    reordered = jnp.moveaxis(array, 0, -2)
    return reordered.reshape(reordered.shape[:-2] + (ELEMS,))


def wall_keep():
    element = jnp.arange(ELEMS)
    wall_layer = (element // ELEM_DEV) % N_WALL
    wall_depth = element % EZ
    at_wall = ((wall_layer == 0) & (wall_depth == 0)).astype(jnp.float32)
    point_level = (jnp.arange(8) == 0).astype(jnp.float32)
    return 1.0 - at_wall[None, None, None, :] * point_level[None, None, :, None]


def shell_coeffs(conductance):
    row_place = jnp.arange(SXG)[:, None]
    up_cond = jnp.concatenate([conductance[1:], conductance[-1:]], axis=0)
    down_cond = jnp.concatenate([conductance[:1], conductance[:-1]], axis=0)
    cond_up = jnp.where(row_place < SXG - 1, 0.5 * (conductance + up_cond), 0.0)
    cond_down = jnp.where(row_place > 0, 0.5 * (conductance + down_cond), 0.0)
    cond_right = 0.5 * (conductance + jnp.roll(conductance, -1, axis=1))
    cond_left = 0.5 * (conductance + jnp.roll(conductance, 1, axis=1))
    return cond_up, cond_down, cond_right, cond_left


def shell_apply(vector, shell_diag, basis_coefficients):
    vec_up = jnp.concatenate([vector[1:], vector[-1:]], axis=0)
    vec_down = jnp.concatenate([vector[:1], vector[:-1]], axis=0)
    vec_right = jnp.roll(vector, -1, axis=1)
    vec_left = jnp.roll(vector, 1, axis=1)
    result = shell_diag * vector + basis_coefficients[0] * (vector - vec_up) + basis_coefficients[1] * (vector - vec_down)
    return result + basis_coefficients[2] * (vector - vec_right) + basis_coefficients[3] * (vector - vec_left)


def reference(temp_in, velocity, spacing, conduct, shell_map, shell_cond, shell_diag):
    weights, matrix = gll_tables()
    point_mass = element_mass(spacing, weights)
    assembled = direct_sum(point_mass)
    keep_mask = wall_keep()
    temp_field = keep_mask * direct_sum(point_mass * temp_in) / assembled

    def rate_of(pieces):
        return element_rate(pieces[0], pieces[1], pieces[2], pieces[3], pieces[4], weights, matrix)

    for substep in range(SUBSTEPS):
        pieces = (to_slabs(temp_field), to_slabs(velocity), to_slabs(spacing), to_slabs(conduct), to_slabs(point_mass))
        rate_term = from_slabs(lax.map(rate_of, pieces))
        temp_field = keep_mask * (temp_field + time_step * direct_sum(rate_term) / assembled)
    temp_out = temp_field

    wall_field = temp_field.reshape((8, 8, 8, N_STREAM, N_SPAN, N_WALL, EX * EY, EZ))[:, :, :, :, :, 0, :, 0]
    wall_field = wall_field.reshape((8, 8, 8, N_STREAM * N_SPAN * EX * EY))
    wall_spacing = spacing.reshape((3, N_STREAM, N_SPAN, N_WALL, EX * EY, EZ))[:, :, :, 0, :, 0]
    wall_spacing = wall_spacing.reshape((3, N_STREAM * N_SPAN * EX * EY))
    wall_conduct = conduct.reshape((N_STREAM, N_SPAN, N_WALL, EX * EY, EZ))[:, :, 0, :, 0].reshape((N_STREAM * N_SPAN * EX * EY,))
    flux = wall_flux(wall_field, wall_spacing, wall_conduct, weights, matrix)
    flux_grid = flux.reshape((8, 8, N_STREAM, N_SPAN, EX, EY)).transpose(0, 1, 2, 4, 3, 5).reshape((8, 8, STREAM_ELEMENTS, SPAN_ELEMENTS))

    owner_dev = shell_map // S_DEV
    node_local = shell_map % S_DEV
    band_index = (jnp.arange(STREAM_ELEMENTS) // EX).astype(jnp.int32)
    sector = (jnp.arange(SPAN_ELEMENTS) // EY).astype(jnp.int32)
    row_place = (band_index[None, None, :, None] * SX + node_local // SY).astype(jnp.int32)
    col_place = ((sector[None, None, None, :] * N_WALL + owner_dev) * SY + node_local % SY).astype(jnp.int32)
    shell_load = jnp.zeros((SXG, SYG), jnp.float32).at[row_place, col_place].add(flux_grid)

    basis_coefficients = shell_coeffs(shell_cond)
    jacobi = shell_diag + basis_coefficients[0] + basis_coefficients[1] + basis_coefficients[2] + basis_coefficients[3]
    shell_temp = jnp.zeros((SXG, SYG), jnp.float32)
    residue = shell_load
    precond = residue / jacobi
    direction = precond
    rz_now = jnp.sum(residue * precond)
    for iteration in range(CG_ITERS):
        applied = shell_apply(direction, shell_diag, basis_coefficients)
        step_len = rz_now / jnp.sum(direction * applied)
        shell_temp = shell_temp + step_len * direction
        residue = residue - step_len * applied
        if iteration + 1 < CG_ITERS:
            precond = residue / jacobi
            rz_next = jnp.sum(residue * precond)
            direction = precond + (rz_next / rz_now) * direction
            rz_now = rz_next
    return temp_out, shell_temp, residue
```

```python
import functools

import jax
import jax.numpy as jnp
import numpy as np
from jax import lax
from jax.experimental import pallas as pl
from jax.experimental.pallas import tpu as pltpu
from jax.sharding import PartitionSpec as P

SUBSTEPS = 2
TIME_STEP = 3e-05
MESH = pl.DeviceIdType.MESH
OFFSETS = [
    (x, y, z) for x in (-1, 0, 1) for y in (-1, 0, 1) for z in (-1, 0, 1) if (x, y, z) != (0, 0, 0)
]
AROUND = [(r, c) for r in (-1, 0, 1) for c in (-1, 0, 1) if (r, c) != (0, 0)]


def face_layout(counts):
    rows, start, total = {}, {}, 0
    for offset in OFFSETS:
        free = sum(1 for d in offset if d == 0)
        rows[offset] = 64 // sum(c for c, d in zip(counts, offset) if d) if free == 2 else 8
        start[offset] = total
        total += rows[offset]
    return rows, start, total


def gll_tables():
    degree = 7
    points = np.array(
        [
            -1.0,
            -0.8717401485096066,
            -0.5917001814331423,
            -0.2092992179024789,
            0.2092992179024789,
            0.5917001814331423,
            0.8717401485096066,
            1.0,
        ]
    )
    previous = np.ones(8)
    current = points.copy()
    for order in range(1, degree):
        following = ((2 * order + 1) * points * current - order * previous) / (order + 1)
        previous = current
        current = following
    weights = 2.0 / (degree * (degree + 1) * current * current)
    differ = points[:, None] - points[None, :]
    safe_differ = np.where(differ == 0.0, 1.0, differ)
    matrix = np.where(differ == 0.0, 0.0, current[:, None] / (current[None, :] * safe_differ))
    matrix[0, 0] = -degree * (degree + 1) / 4.0
    matrix[degree, degree] = degree * (degree + 1) / 4.0
    return weights, matrix


WEIGHTS, MATRIX = gll_tables()
STIFF = (MATRIX.T * WEIGHTS[None, :]) @ MATRIX / WEIGHTS[:, None]


def mxu_tables():
    parts = []
    eye4, eye8, eye32 = np.eye(4), np.eye(8), np.eye(32)
    for table in (MATRIX, STIFF):
        parts.append(np.kron(eye4, np.kron(table, eye8)))
    for table in (MATRIX, STIFF):
        parts.append(np.kron(eye32, table))
    whole = np.concatenate(parts, axis=0).astype(np.float32)
    high = whole.astype(jnp.bfloat16)
    low = (whole - high.astype(np.float32)).astype(jnp.bfloat16)
    return np.concatenate([high, high, low], axis=1)


def side(d):
    return 7 if d > 0 else 0


def roll(value, shift, axis):
    size = value.shape[axis]
    shift = shift % size
    return value if shift == 0 else pltpu.roll(value, shift, axis)


def kernel(
    dims,
    temp_hbm, vel_hbm, lhs_hbm, spacing_hbm, conduct_hbm, map_hbm, cond_hbm, diag_hbm,
    out_temp, out_shell, out_resid,
    temp_ref, vel, LHS, spacing_ref, conduct_ref, map_ref, cond_ref, diag_ref,
    T0, T, R, MASS, INVA,
    send0, recv0, send1, recv1, send2, recv2,
    part_send, edge_send, area_send, part_buf, edge_buf, area_buf,
    Bt, Am, stat_send, stat_buf, sum_send, sum_buf,
    face_ssem, face_rsem, part_ssem, part_rsem, edge_rsem, area_ssem, area_rsem,
    st_ssem, st_rsem, p_ssem, p_rsem, loc_sem,
):
    NS, NP, NW, EX, EY, EZ = dims
    N = NS * NP * NW
    SX, SY = cond_ref.shape
    lanes = EX * EY * EZ
    s = lax.axis_index("stream")
    p = lax.axis_index("span")
    w = lax.axis_index("wall")
    me = (s * NP + p) * NW + w
    f32 = jnp.float32

    rows_of, START, _ = face_layout((EX, EY, EZ))

    def wrapped(index, size):
        return [index] + [
            jnp.where(index + d >= size, index + d - size, index + d) for d in range(1, size)
        ]

    s_of = wrapped(s, NS) if NS <= 4 else None
    p_of, w_of = wrapped(p, NP), wrapped(w, NW)
    s_up = jnp.where(s + 1 >= NS, 0, s + 1)
    s_down = jnp.where(s == 0, NS - 1, s - 1)
    s_near = (s, s_up, s_down)
    p_near = (p, p_of[1], p_of[NP - 1])
    w_near = (w, w_of[1], w_of[NW - 1])

    def everyone(visit):
        def plane(ds, s_there):
            for dp in reversed(range(NP)):
                for dw in reversed(range(NW)):
                    if isinstance(ds, int) and (ds, dp, dw) == (0, 0, 0):
                        continue
                    visit((ds * NP + dp) * NW + dw - 1, (s_there, p_of[dp], w_of[dw]))

        if s_of is not None:
            for ds in reversed(range(1, NS)):
                plane(ds, s_of[ds])
        else:
            def step(ds, _):
                plane(ds, jnp.where(s + ds >= NS, s + ds - NS, s + ds))
                return 0

            lax.fori_loop(1, NS, step, 0)
        plane(0, s)

    barrier = pltpu.get_barrier_semaphore()

    loads = [
        pltpu.make_async_copy(source, target, loc_sem.at[n])
        for n, (source, target) in enumerate(
            (
                (spacing_hbm, spacing_ref), (conduct_hbm, conduct_ref), (temp_hbm, temp_ref),
                (cond_hbm, cond_ref), (diag_hbm, diag_ref), (map_hbm, map_ref),
                (vel_hbm, vel), (lhs_hbm, LHS),
            )
        )
    ]
    for load_ in loads:
        load_.start()
    everyone(
        lambda slot, there: pl.semaphore_signal(
            barrier, inc=1, device_id=there, device_id_type=MESH
        )
    )
    lane = lax.broadcasted_iota(jnp.int32, (1, lanes), 1)
    la = lane // (EY * EZ)
    lb = lane // EZ % EY
    lc = lane % EZ
    sub = lax.broadcasted_iota(jnp.int32, (8, lanes), 0)

    def column(values):
        result = jnp.full((8, lanes), float(values[0]), f32)
        for k in range(1, 8):
            result = jnp.where(sub == k, float(values[k]), result)
        return result

    def exists(ds, dw):
        conds = []
        if ds:
            conds.append((s + ds >= 0) & (s + ds < NS))
        if dw:
            conds.append((w + dw >= 0) & (w + dw < NW))
        if not conds:
            return None
        return conds[0] if len(conds) == 1 else conds[0] & conds[1]

    def under(cond, body):
        if cond is None:
            body()
        else:
            pl.when(cond)(body)

    for load_ in loads[:3]:
        load_.wait()
    sp0, sp1, sp2 = spacing_ref[0:1, :], spacing_ref[1:2, :], spacing_ref[2:3, :]
    conduct = conduct_ref[...]
    sx, sy, sz = 2.0 / sp0, 2.0 / sp1, 2.0 / sp2
    wk = column(WEIGHTS)
    mass_kn = wk * (sp0 * sp1 * sp2 / 8.0)
    for i in range(8):
        for j in range(8):
            m = float(WEIGHTS[i] * WEIGHTS[j]) * mass_kn
            MASS[i, j] = m
            T0[1, i, j] = m
            T0[0, i, j] = m * temp_ref[i, j]
    def view(field, ch, offset):
        return tuple([ch] + [slice(None) if d == 0 else side(d) for d in offset])

    axes = ((la, EX, EY * EZ), (lb, EY, EZ), (lc, EZ, 1))

    def local_assemble(field, channels):
        for ch in range(channels):
            for axis, (step, place, count) in enumerate(
                ((EY * EZ, la, EX), (EZ, lb, EY), (1, lc, EZ))
            ):
                lo = [ch, slice(None), slice(None), slice(None)]
                hi = list(lo)
                lo[axis + 1], hi[axis + 1] = 0, 7
                lo, hi = tuple(lo), tuple(hi)
                f0 = field[lo].reshape(64, lanes)
                f7 = field[hi].reshape(64, lanes)
                n7 = f7 + jnp.where(place < count - 1, roll(f0, -step, 1), 0.0)
                n0 = f0 + jnp.where(place > 0, roll(f7, step, 1), 0.0)
                field[lo] = n0.reshape(8, 8, lanes)
                field[hi] = n7.reshape(8, 8, lanes)

    def descriptor(rnd, send, recv, index):
        offset = OFFSETS[index]
        rows = pl.ds(START[offset], rows_of[offset])
        return pltpu.make_async_remote_copy(
            src_ref=send.at[:, rows, :],
            dst_ref=recv.at[:, rows, :],
            send_sem=face_ssem.at[rnd, index],
            recv_sem=face_rsem.at[rnd, index],
            device_id=(s_near[offset[0]], p_near[offset[1]], w_near[offset[2]]),
            device_id_type=MESH,
        )

    order = sorted(range(len(OFFSETS)), key=lambda i: -sum(1 for d in OFFSETS[i] if d))

    groups_to = {}
    for index in order:
        groups_to.setdefault((OFFSETS[index][0], OFFSETS[index][2]), []).append(index)

    def send_faces(rnd, field, channels, send, recv):
        for index in order:
            offset = OFFSETS[index]
            n_rows = rows_of[offset]
            free = sum(1 for d in offset if d == 0)
            for ch in range(channels):
                if free == 0:
                    i, j, k = [side(d) for d in offset]
                    value = jnp.broadcast_to(field[ch, i, j, k : k + 1, :], (8, lanes))
                elif free == 1:
                    value = field[view(field, ch, offset)]
                else:
                    face = field[view(field, ch, offset)].reshape(64, lanes)
                    axis = [n for n in range(3) if offset[n]][0]
                    place, count, step = axes[axis]
                    own = count - 1 if offset[axis] > 0 else 0
                    value = roll(face[0:n_rows], -own * step, 1)
                    for g in range(1, count):
                        piece = roll(face[g * n_rows : (g + 1) * n_rows], (g - own) * step, 1)
                        value = jnp.where(place == g, piece, value)
                send[ch, START[offset] : START[offset] + n_rows, :] = value
        if rnd == 0:
            pl.semaphore_wait(barrier, N - 1)
        for (ds, dw), indices in groups_to.items():
            def body(indices=indices):
                for index in indices:
                    descriptor(rnd, send, recv, index).start()

            under(exists(ds, dw), body)

    def take_faces(rnd, field, channels, send, recv):
        for (ds, dw), indices in groups_to.items():
            def body(indices=indices):
                for index in indices:
                    descriptor(rnd, send, recv, index).wait_recv()

            under(exists(-ds, -dw), body)
        for index in reversed(order):
            offset = OFFSETS[index]
            n_rows = rows_of[offset]
            free = sum(1 for d in offset if d == 0)
            back = tuple(-d for d in offset)
            shift = 0
            mask = None
            for d, (place, count, step) in zip(offset, axes):
                if d:
                    shift -= d * (count - 1) * step
                    here = place == (0 if d > 0 else count - 1)
                    mask = here if mask is None else mask & here
            there = exists(back[0], back[2])
            if there is not None:
                mask = mask & there
            start = START[offset]
            for ch in range(channels):
                value = recv[ch, start : start + n_rows, :]
                if free == 2:
                    axis = [n for n in range(3) if back[n]][0]
                    place, count, step = axes[axis]
                    own = count - 1 if back[axis] > 0 else 0
                    value = jnp.concatenate(
                        [roll(value, (own - g) * step, 1) for g in range(count)], axis=0
                    )
                else:
                    value = roll(value, shift, 1)
                value = jnp.where(mask, value, 0.0)
                if free == 0:
                    i, j, k = [side(d) for d in back]
                    field[ch, i, j, k : k + 1, :] = field[ch, i, j, k : k + 1, :] + value[0:1]
                else:
                    spot = view(field, ch, back)
                    old = field[spot]
                    field[spot] = old + value.reshape(old.shape)

    def drain_faces(rnd, send, recv):
        for index in order:
            offset = OFFSETS[index]

            def body(index=index):
                descriptor(rnd, send, recv, index).wait_send()

            under(exists(offset[0], offset[2]), body)

    groups = 64 // EZ
    s_dev = SX * SY
    half = groups // 2
    owners = 3 * SX
    reach = min(2, NS - 1)
    near = min(1, reach)
    edge = (w == 0) | (w == NW - 1)
    toward = jnp.where(w == 0, -1, 1)

    def split(value, size):
        if size & (size - 1):
            return value // size, value % size
        return lax.shift_right_logical(value, size.bit_length() - 1), value & (size - 1)

    local_assemble(T0, 2)
    for load_ in loads[3:6]:
        load_.wait()
    stat_send[0:SX] = cond_ref[...]
    stat_send[SX : 2 * SX] = diag_ref[...]

    codes = []
    for a in range(EX):
        t = map_ref[:, :, a, :].reshape(64, EY)
        owner, node = split(t, s_dev)
        row, col = split(node, SY)
        codes += [(owner * SX + row).astype(f32), col.astype(f32)]
    bi = lax.broadcasted_iota(jnp.int32, (EY, lanes), 0)
    spread = jnp.where(bi == lb, 1.0, 0.0).astype(jnp.bfloat16)
    spreads = jnp.dot(
        jnp.concatenate(codes, axis=0).astype(jnp.bfloat16), spread, preferred_element_type=f32
    )
    picked = []
    for part in range(2):
        full = spreads[part * 64 : (part + 1) * 64]
        for a in range(1, EX):
            full = jnp.where(
                la == a, spreads[(2 * a + part) * 64 : (2 * a + part + 1) * 64], full
            )
        packed = full[0:groups]
        for g in range(1, EZ):
            packed = jnp.where(lc == g, full[g * groups : (g + 1) * groups], packed)
        picked.append(packed)
    stat_send[2 * SX : 2 * SX + groups] = picked[0] * float(SY) + picked[1]

    area = jnp.where(lc == 0, conduct * sz * (sp0 * sp1 / 4.0), 0.0)
    for step in range(EZ.bit_length() - 1):
        area = area + roll(area, 1 << step, 1)
    area_send[...] = jnp.broadcast_to(area, (8, lanes))

    @pl.when(w == 0)
    def _():
        area_buf[near, 0] = area_send[...]


    qi = lax.broadcasted_iota(jnp.int32, (SY, lanes), 0)
    ri = lax.broadcasted_iota(jnp.int32, (owners, lanes), 0)

    def scatter_table(band, kind, code):
        code = code.astype(jnp.int32)
        row, col = split(code, SY)
        shift = SX - SX * w
        if kind:
            shift = shift + toward * (SX * NW)
        row = row + shift
        for g in range(groups):
            at = slice((kind * groups + g) * lanes, (kind * groups + g + 1) * lanes)
            Bt[band, :, at] = jnp.where(qi == col[g : g + 1], 1.0, 0.0).astype(jnp.bfloat16)
            Am[band, :, at] = jnp.where(ri == row[g : g + 1], 1.0, 0.0)

    scatter_table(near, 0, picked[0] * float(SY) + picked[1])

    def receivers(visit, wanted):
        for ds in range(-reach, reach + 1):
            def body(ds=ds):
                for there in range(NW):
                    if there == 0:
                        plan = [(0, 0), (-1, 1), (1, -1), (-2, 2)]
                    elif there == NW - 1:
                        plan = [(0, 0), (1, 1), (-1, -1), (2, 2)]
                    else:
                        plan = [(0, 0), (-1, -1), (1, 1)]
                    for turn, (dp, place) in enumerate(plan):
                        full = dp == 0 or (place == 1 and there in (0, NW - 1))
                        if not wanted(full, ds) or (ds, dp, there) == (0, 0, 0):
                            continue
                        index = ((ds + reach) * NW + there) * 4 + turn
                        visit(full, ds, place, (s - ds, p_of[(-dp) % NP], there), index)

            under(exists(-ds, 0), body)

    def part_copy(ds, place, there=None, index=0):
        return pltpu.make_async_remote_copy(
            src_ref=part_send, dst_ref=part_buf.at[ds + reach, place],
            send_sem=part_ssem.at[index], recv_sem=part_rsem.at[ds + reach, place],
            device_id=(s, p, 0) if there is None else there, device_id_type=MESH,
        )

    def edge_copy(ds, place, there=None, index=0):
        return pltpu.make_async_remote_copy(
            src_ref=edge_send, dst_ref=edge_buf.at[ds + reach, place + 1],
            send_sem=part_ssem.at[index], recv_sem=edge_rsem.at[ds + reach, place + 1],
            device_id=(s, p, 0) if there is None else there, device_id_type=MESH,
        )

    def area_copy(ds, place, there=None, index=0):
        return pltpu.make_async_remote_copy(
            src_ref=area_send, dst_ref=area_buf.at[ds + near, place],
            send_sem=area_ssem.at[index], recv_sem=area_rsem.at[ds + near, place],
            device_id=(s, p, 0) if there is None else there, device_id_type=MESH,
        )

    def send_parts(what):
        def visit(full, ds, place, there, index):
            copy = (part_copy if full else edge_copy)(ds, place, there, index)
            copy.start() if what == "start" else copy.wait_send()

        receivers(visit, lambda full, ds: True)

    def send_areas(what):
        def visit(full, ds, place, there, index):
            copy = area_copy(ds, place, there, index)
            copy.start() if what == "start" else copy.wait_send()

        receivers(visit, lambda full, ds: full and abs(ds) <= near)

    def take(copy_of, ds, places):
        for place in places:
            copy_of(ds, place).wait_recv()

    def take_all(copy_of, bands, main, side, sides):
        for ds in bands:
            def body(ds=ds):
                if ds:
                    take(copy_of, ds, main)
                else:
                    pl.when(w != 0)(lambda: take(copy_of, ds, main))
                pl.when(edge)(lambda: take(copy_of, ds, side))
                if sides:
                    pl.when(jnp.logical_not(edge))(lambda: take(copy_of, ds, sides))

            under(exists(ds, 0), body)

    send_faces(0, T0, 2, send0, recv0)

    ring = NP * NW
    spot_c = p * NW + w
    ring_up = jnp.where(spot_c == ring - 1, 0, spot_c + 1)
    ring_down = jnp.where(spot_c == 0, ring - 1, spot_c - 1)
    q_at = {1: (ring_up // NW, ring_up % NW), 0: (p, w), -1: (ring_down // NW, ring_down % NW)}

    def patch_copy(index):
        dr, dc = AROUND[index]
        slot = (1 - dr) * 3 + (1 - dc)
        return pltpu.make_async_remote_copy(
            src_ref=stat_send,
            dst_ref=stat_buf.at[slot],
            send_sem=st_ssem.at[index],
            recv_sem=st_rsem.at[index],
            device_id=(s_near[dr],) + q_at[dc],
            device_id_type=MESH,
        )

    def patches(what):
        for index, (dr, dc) in enumerate(AROUND):
            def body(index=index):
                copy = patch_copy(index)
                if what == "start":
                    copy.start()
                elif what == "recv":
                    copy.wait_recv()
                else:
                    copy.wait_send()

            under(exists(-dr if what == "recv" else dr, 0), body)

    patches("start")
    pl.when(w == 0)(lambda: send_areas("start"))
    for slot in range(9):
        dr = slot // 3 - 1
        if dr:
            @pl.when(jnp.logical_not(exists(dr, 0)))
            def _(slot=slot):
                stat_buf[slot] = jnp.ones(stat_send.shape, f32)
    stat_buf[4] = stat_send[...]

    keep_lane = jnp.where((lc == 0) & (w == 0), 0.0, 1.0)
    keep = jnp.where(sub == 0, jnp.broadcast_to(keep_lane, (8, lanes)), 1.0)

    take_faces(0, T0, 2, send0, recv0)
    for i in range(8):
        inv = keep / T0[1, i]
        T[0, i] = T0[0, i] * inv
        INVA[i] = inv * TIME_STEP
    for load_ in loads[6:]:
        load_.wait()

    cxx, cyy, czz = conduct * sx, conduct * sy, conduct * sz

    def other_tables():
        patches("recv")
        for ds in range(-near, near + 1):
            for kind in range(2):
                if (ds, kind) == (0, 0):
                    continue
                slot = (ds + 1) * 3 + 1 + (toward if kind else 0)
                scatter_table(ds + near, kind, stat_buf[slot, 2 * SX : 2 * SX + groups])

    def wall_part():
        shared = jnp.where((sub == 0) & (lb == 0), 0.5, 1.0)
        shared = jnp.where((sub == 7) & (lb == EY - 1), 0.5, shared)
        rows = []
        for i in range(8):
            mine = float(MATRIX[0, 1]) * T[0, i, :, 1, :]
            rate = float(MATRIX[0, 1]) * (R[0, i, :, 1, :] * INVA[i, :, 1, :])
            for m in range(2, 8):
                mine = mine + float(MATRIX[0, m]) * T[0, i, :, m, :]
                rate = rate + float(MATRIX[0, m]) * (R[0, i, :, m, :] * INVA[i, :, m, :])
            weight = shared
            if i == 0:
                weight = jnp.where((la == 0) & (s > 0), 0.5 * shared, shared)
            elif i == 7:
                weight = jnp.where((la == EX - 1) & (s < NS - 1), 0.5 * shared, shared)
            rows.append(jnp.where(lc == 0, mine * weight + rate, 0.0))
        flat = jnp.concatenate(rows, axis=0)
        packed = flat[0:groups]
        for g in range(1, EZ):
            packed = packed + roll(flat[g * groups : (g + 1) * groups], g, 1)
        part_send[...] = packed
        edge_send[...] = jnp.where(
            (sub == 0) | (sub == 7), packed[0:half], roll(packed[half:groups], 2, 0)
        )
        part_buf[reach, 0] = packed
        send_parts("start")

    for rnd in range(1, SUBSTEPS + 1):
        send, recv = (send1, recv1) if rnd == 1 else (send2, recv2)
        def terms(get, top, bottom):
            value = jnp.concatenate(
                [jnp.concatenate([get(4 * h + q) for q in range(4)], axis=0) for h in range(2)],
                axis=1,
            )
            high = value.astype(jnp.bfloat16)
            low = (value - high.astype(f32)).astype(jnp.bfloat16)
            rhs = jnp.concatenate([high, low, high], axis=0)
            return jnp.dot(LHS[top:bottom, :], rhs, preferred_element_type=f32)

        def piece(found, kind, at):
            rows = kind * 256 + (at % 4) * 64
            cols = (at // 4) * lanes
            return found[rows : rows + 64, cols : cols + lanes].reshape(8, 8, lanes)

        along = terms(lambda j: T[0, :, j].reshape(64, lanes), 0, 512)
        for j in range(8):
            grad, stiff = piece(along, 0, j), piece(along, 1, j)
            R[0, :, j] = sx * (vel[0, :, j].astype(f32) * grad + cxx * stiff)
        across = terms(lambda i: T[0, i].reshape(64, lanes), 0, 1024)
        for i in range(8):
            total = R[0, i]
            total = total + sy * (
                vel[1, i].astype(f32) * piece(across, 0, i) + cyy * piece(across, 1, i)
            )
            total = total + sz * (
                vel[2, i].astype(f32) * piece(across, 2, i) + czz * piece(across, 3, i)
            )
            R[0, i] = -(MASS[i] * total)
        local_assemble(R, 1)
        if rnd == SUBSTEPS:
            pl.when(w == 0)(lambda: wall_part())
        send_faces(rnd, R, 1, send, recv)
        if rnd < SUBSTEPS:
            if rnd == 1:
                other_tables()
            take_faces(rnd, R, 1, send, recv)
            for a in range(8):
                T[0, a] = keep * T[0, a] + R[0, a] * INVA[a]

    def wide(get):
        return jnp.concatenate(
            [jnp.concatenate([get(3 * r + c) for c in range(3)], axis=1) for r in range(3)], axis=0
        )

    cond = wide(lambda slot: stat_buf[slot, 0:SX])
    diag = wide(lambda slot: stat_buf[slot, SX : 2 * SX])
    grow = s * SX - SX + lax.broadcasted_iota(jnp.int32, cond.shape, 0)
    cup = jnp.where(grow != NS * SX - 1, 0.5 * (cond + roll(cond, -1, 0)), 0.0)
    cdown = jnp.where(grow != 0, 0.5 * (cond + roll(cond, 1, 0)), 0.0)
    cright = 0.5 * (cond + roll(cond, -1, 1))
    cleft = 0.5 * (cond + roll(cond, 1, 1))
    jacobi = diag + cup + cdown + cright + cleft
    inv_jacobi = 1.0 / jacobi

    def apply(v):
        return (
            jacobi * v
            - cup * roll(v, -1, 0)
            - cdown * roll(v, 1, 0)
            - cright * roll(v, -1, 1)
            - cleft * roll(v, 1, 1)
        )

    def centre(v):
        return v[SX : 2 * SX, SY : 2 * SY]

    point = lax.broadcasted_iota(jnp.int32, (groups, lanes), 0) + lc * groups
    wi = jnp.full((groups, lanes), float(WEIGHTS[0]), f32)
    wj = jnp.full((groups, lanes), float(WEIGHTS[0]), f32)
    for k in range(1, 8):
        wi = jnp.where(point // 8 == k, float(WEIGHTS[k]), wi)
        wj = jnp.where(point % 8 == k, float(WEIGHTS[k]), wj)
    wij = wi * wj

    take_all(area_copy, range(-near, near + 1), (0,), (1,), ())
    bands = range(-reach, reach + 1)
    take_all(part_copy, bands, (0,), (1,), ())
    take_all(edge_copy, bands, (), (-1, 2), (-1, 1))

    def both(mask, cond):
        return mask if cond is None else mask & cond

    def edge_rows(part):
        return jnp.where(
            (sub == 0) | (sub == 7), part[0:half], roll(part[half:groups], 2, 0)
        )

    def span_sum(part, above, below):
        above = roll(above, (EY - 1) * EZ, 1)
        below = roll(below, -(EY - 1) * EZ, 1)
        high = (sub == 7) & (lb == EY - 1)
        low = (sub == 0) & (lb == 0)
        rows = []
        for h, (first, last) in enumerate(((0, 7), (2, 1))):
            rows.append(
                part[h * half : (h + 1) * half]
                + jnp.where(high, above[first : first + 1], 0.0)
                + jnp.where(low, below[last : last + 1], 0.0)
            )
        return rows

    summed = {}
    for ds in bands:
        mains, sides = part_buf[ds + reach, 0], part_buf[ds + reach, 1]
        back, ahead, far = [edge_buf[ds + reach, place + 1] for place in (-1, 1, 2)]
        main_edge = edge_rows(mains)
        ahead = jnp.where(edge, edge_rows(sides), ahead)
        up = toward > 0
        summed[ds, 0] = span_sum(mains, jnp.where(up, ahead, back), jnp.where(up, back, ahead))
        summed[ds, 1] = span_sum(
            sides, jnp.where(up, far, main_edge), jnp.where(up, main_edge, far)
        )
    jump = (EX - 1) * EY * EZ + EZ - 1
    loads_wide = []
    for ds in range(-1, 2):
        if abs(ds) > near:
            loads_wide.append(jnp.zeros((SX, owners * SY // SX), f32))
            continue
        here = exists(ds, 0)
        lhs = []
        for kind in range(2):
            even, odd = summed[ds, kind]
            if ds + 1 <= reach:
                more = roll(summed[ds + 1, kind][0], jump, 1)
                odd = odd + jnp.where(
                    both((la == EX - 1) & (lc == EZ - 1), exists(ds + 1, 0)), more, 0.0
                )
            if ds - 1 >= -reach:
                more = roll(summed[ds - 1, kind][1], -jump, 1)
                even = even + jnp.where(both((la == 0) & (lc == 0), exists(ds - 1, 0)), more, 0.0)
            scale = area_buf[ds + near, kind]
            flux = jnp.concatenate([even * scale, odd * scale], axis=0) * wij
            valid = edge if kind else None
            if here is not None:
                valid = here if valid is None else valid & here
            if valid is not None:
                flux = jnp.where(valid, flux, 0.0)
            high = flux.astype(jnp.bfloat16).astype(f32)
            for piece_ in (high, flux - high):
                lhs.append(
                    Am[ds + near, :, kind * groups * lanes : (kind + 1) * groups * lanes]
                    * jnp.concatenate(
                        [
                            jnp.broadcast_to(piece_[g : g + 1], (owners, lanes))
                            for g in range(groups)
                        ],
                        axis=1,
                    )
                )
        lhs = jnp.concatenate(
            [
                jnp.concatenate([lhs[0], lhs[2]], axis=1),
                jnp.concatenate([lhs[1], lhs[3]], axis=1),
            ],
            axis=0,
        ).astype(jnp.bfloat16)
        found = lax.dot_general(
            lhs, Bt[ds + near], (((1,), (1,)), ((), ())), preferred_element_type=f32
        )
        found = found[0:owners] + found[owners : 2 * owners]
        loads_wide.append(
            jnp.concatenate([found[c * SX : (c + 1) * SX] for c in range(3)], axis=1)
        )
    load_wide = jnp.concatenate(loads_wide, axis=0)
    load = centre(load_wide)
    z_wide = load_wide * inv_jacobi
    z_mine = centre(z_wide)
    image_wide = apply(z_wide)
    y_wide = image_wide * inv_jacobi
    ay = centre(apply(y_wide))
    image = centre(image_wide)
    y = centre(y_wide)

    def rowsum(v):
        return jnp.sum(v, axis=0, keepdims=True)

    fourth = SY // 4
    line = lax.broadcasted_iota(jnp.int32, (1, SY), 1) // fourth

    def folded(v):
        v = rowsum(v)
        v = v + roll(v, SY // 2, 1)
        return v + roll(v, SY // 4, 1)

    mine = folded(load * z_mine)
    for place, product in enumerate((z_mine * image, image * y, y * ay)):
        mine = jnp.where(line == place + 1, folded(product), mine)
    sum_send[...] = mine
    sum_buf[N - 1 : N, :] = mine

    def sum_copy(slot, there):
        return pltpu.make_async_remote_copy(
            src_ref=sum_send,
            dst_ref=sum_buf.at[pl.ds(slot, 1), :],
            send_sem=p_ssem.at[0],
            recv_sem=p_rsem.at[0],
            device_id=there,
            device_id_type=MESH,
        )

    everyone(lambda slot, there: sum_copy(slot, there).start())

    take_faces(SUBSTEPS, R, 1, send2, recv2)
    for a in range(8):
        out_temp[a] = keep * T[0, a] + R[0, a] * INVA[a]

    for rnd, (send, recv) in enumerate(((send0, recv0), (send1, recv1), (send2, recv2))):
        drain_faces(rnd, send, recv)
    patches("send")

    @pl.when(w == 0)
    def _():
        send_areas("send")
        send_parts("send")

    arrived = sum_buf.at[pl.ds(0, N - 1), :]
    pltpu.make_async_copy(arrived, arrived, p_ssem.at[0]).wait()
    pltpu.make_async_copy(arrived, arrived, p_rsem.at[0]).wait()
    totals = jnp.sum(sum_buf[...], axis=0, keepdims=True)
    rz, curve, m, q = [
        jnp.sum(jnp.where(line == place, totals, 0.0), axis=1, keepdims=True) for place in range(4)
    ]
    alpha = rz / curve
    new = alpha * alpha * m - rz
    beta = new / rz
    one = 1.0 + beta
    curve_next = one * one * curve - 2.0 * one * alpha * m + alpha * alpha * q
    alpha_next = new / curve_next
    direction = one * z_mine - alpha * y
    out_shell[...] = alpha * z_mine + alpha_next * direction
    out_resid[...] = load - alpha * image - alpha_next * (one * image - alpha * ay)


def hand_over(a_ref, b_ref, c_ref, x_ref, y_ref, z_ref):
    x_ref[...] = a_ref[...]
    y_ref[...] = b_ref[...]
    z_ref[...] = c_ref[...]


def per_device(sizes, temp_in, velocity, spacing, conduct, shell_map, shell_cond, shell_diag):
    NS, NP, NW = sizes
    N = NS * NP * NW
    lanes = temp_in.shape[3]
    EX, EY = shell_map.shape[2:]
    EZ = lanes // (EX * EY)
    groups = 64 // EZ
    reach = min(2, NS - 1)
    near = min(1, reach)
    SX, SY = shell_cond.shape
    assert lanes == SY and groups == 16 and NP > 2 and NW > 1
    ROWS = face_layout((EX, EY, EZ))[2]
    lhs = jnp.asarray(mxu_tables())
    f32 = jnp.float32
    block = (8, 8, 8, lanes)
    vmem = pl.BlockSpec(memory_space=pltpu.VMEM)
    V = pltpu.VMEM
    dma = pltpu.SemaphoreType.DMA
    outs = pl.pallas_call(
        functools.partial(kernel, (NS, NP, NW, EX, EY, EZ)),
        out_shape=(
            pltpu.VMEM(block, f32),
            pltpu.VMEM((SX, SY), f32),
            pltpu.VMEM((SX, SY), f32),
        ),
        in_specs=[pl.BlockSpec(memory_space=pltpu.HBM)] * 8,
        out_specs=(vmem, vmem, vmem),
        scratch_shapes=[
            V(block, f32), V((3,) + block, jnp.bfloat16), V(lhs.shape, jnp.bfloat16),
            V((3, lanes), f32), V((1, lanes), f32), V(shell_map.shape, jnp.int32),
            V((SX, SY), f32), V((SX, SY), f32),
            V((2,) + block, f32), V((1,) + block, f32), V((1,) + block, f32),
            V(block, f32), V(block, f32),
            V((2, ROWS, lanes), f32), V((2, ROWS, lanes), f32),
            V((1, ROWS, lanes), f32), V((1, ROWS, lanes), f32),
            V((1, ROWS, lanes), f32), V((1, ROWS, lanes), f32),
            V((groups, lanes), f32), V((8, lanes), f32), V((8, lanes), f32),
            V((2 * reach + 1, 2, groups, lanes), f32), V((2 * reach + 1, 4, 8, lanes), f32),
            V((2 * near + 1, 2, 8, lanes), f32),
            V((2 * near + 1, SY, 2 * groups * lanes), jnp.bfloat16),
            V((2 * near + 1, 3 * SX, 2 * groups * lanes), f32),
            V((2 * SX + groups, SY), f32), V((9, 2 * SX + groups, SY), f32),
            V((1, SY), f32), V((N, SY), f32),
            dma((3, len(OFFSETS))), dma((3, len(OFFSETS))),
            dma(((2 * reach + 1) * NW * 4,)), dma((2 * reach + 1, 2)), dma((2 * reach + 1, 4)),
            dma(((2 * reach + 1) * NW * 4,)), dma((2 * near + 1, 2)),
            dma((8,)), dma((8,)), dma((1,)), dma((1,)), dma((8,)),
        ],
        compiler_params=pltpu.CompilerParams(
            collective_id=0, has_side_effects=True, vmem_limit_bytes=24 << 20
        ),
    )(
        *[
            pltpu.with_memory_space_constraint(x, pltpu.HBM)
            for x in (
                temp_in, velocity, lhs, spacing, conduct.reshape(1, lanes), shell_map, shell_cond,
                shell_diag,
            )
        ]
    )
    return pl.pallas_call(
        hand_over,
        out_shape=tuple(jax.ShapeDtypeStruct(o.shape, o.dtype) for o in outs),
        in_specs=[vmem] * 3,
        out_specs=(vmem,) * 3,
        compiler_params=pltpu.CompilerParams(vmem_limit_bytes=4 << 20),
    )(*outs)


def solution(mesh):
    sizes = (mesh.shape["stream"], mesh.shape["span"], mesh.shape["wall"])
    return jax.shard_map(
        functools.partial(per_device, sizes),
        mesh=mesh,
        in_specs=(
            P(None, None, None, ("stream", "span", "wall")),
            P(None, None, None, None, ("stream", "span", "wall")),
            P(None, ("stream", "span", "wall")),
            P(("stream", "span", "wall")),
            P(None, None, "stream", "span"),
            P("stream", ("span", "wall")),
            P("stream", ("span", "wall")),
        ),
        out_specs=(
            P(None, None, None, ("stream", "span", "wall")),
            P("stream", ("span", "wall")),
            P("stream", ("span", "wall")),
        ),
        check_vma=False,
    )
```

```python
import functools

import jax
import jax.numpy as jnp
import numpy as np
from jax import lax
from jax.experimental import pallas as pl
from jax.experimental.pallas import tpu as pltpu
from jax.sharding import PartitionSpec as P

SUBSTEPS = 2
TIME_STEP = 3e-05
MESH = pl.DeviceIdType.MESH
OFFSETS = [
    (x, y, z) for x in (-1, 0, 1) for y in (-1, 0, 1) for z in (-1, 0, 1) if (x, y, z) != (0, 0, 0)
]
AROUND = [(r, c) for r in (-1, 0, 1) for c in (-1, 0, 1) if (r, c) != (0, 0)]


def face_layout(counts):
    rows, start, total = {}, {}, 0
    for offset in OFFSETS:
        free = sum(1 for d in offset if d == 0)
        rows[offset] = 64 // sum(c for c, d in zip(counts, offset) if d) if free == 2 else 8
        start[offset] = total
        total += rows[offset]
    return rows, start, total


def gll_tables():
    degree = 7
    points = np.array(
        [
            -1.0,
            -0.8717401485096066,
            -0.5917001814331423,
            -0.2092992179024789,
            0.2092992179024789,
            0.5917001814331423,
            0.8717401485096066,
            1.0,
        ]
    )
    previous = np.ones(8)
    current = points.copy()
    for order in range(1, degree):
        following = ((2 * order + 1) * points * current - order * previous) / (order + 1)
        previous = current
        current = following
    weights = 2.0 / (degree * (degree + 1) * current * current)
    differ = points[:, None] - points[None, :]
    safe_differ = np.where(differ == 0.0, 1.0, differ)
    matrix = np.where(differ == 0.0, 0.0, current[:, None] / (current[None, :] * safe_differ))
    matrix[0, 0] = -degree * (degree + 1) / 4.0
    matrix[degree, degree] = degree * (degree + 1) / 4.0
    return weights, matrix


WEIGHTS, MATRIX = gll_tables()
STIFF = (MATRIX.T * WEIGHTS[None, :]) @ MATRIX / WEIGHTS[:, None]


def mxu_tables():
    parts = []
    eye4, eye8, eye32 = np.eye(4), np.eye(8), np.eye(32)
    for table in (MATRIX, STIFF):
        parts.append(np.kron(eye4, np.kron(table, eye8)))
    for table in (MATRIX, STIFF):
        parts.append(np.kron(eye32, table))
    whole = np.concatenate(parts, axis=0).astype(np.float32)
    high = whole.astype(jnp.bfloat16)
    low = (whole - high.astype(np.float32)).astype(jnp.bfloat16)
    return np.concatenate([high, high, low], axis=1)


def side(d):
    return 7 if d > 0 else 0


def roll(value, shift, axis):
    size = value.shape[axis]
    shift = shift % size
    return value if shift == 0 else pltpu.roll(value, shift, axis)


def kernel(
    dims,
    temp_hbm, vel_hbm, lhs_hbm, spacing_hbm, conduct_hbm, map_hbm, cond_hbm, diag_hbm,
    out_temp, out_shell, out_resid,
    temp_ref, vel, LHS, spacing_ref, conduct_ref, map_ref, cond_ref, diag_ref,
    T0, T, R, MASS, INVA,
    send0, recv0, send1, recv1, send2, recv2,
    part_send, edge_send, area_send, part_buf, edge_buf, area_buf,
    Bt, Am, Am_other, Side, stat_send, stat_buf, sum_send, sum_buf,
    face_ssem, face_rsem, part_ssem, part_rsem, edge_rsem, area_ssem, area_rsem,
    st_ssem, st_rsem, p_ssem, p_rsem, loc_sem,
):
    NS, NP, NW, EX, EY, EZ = dims
    N = NS * NP * NW
    SX, SY = cond_ref.shape
    lanes = EX * EY * EZ
    s = lax.axis_index("stream")
    p = lax.axis_index("span")
    w = lax.axis_index("wall")
    me = (s * NP + p) * NW + w
    f32 = jnp.float32

    rows_of, START, _ = face_layout((EX, EY, EZ))

    def wrapped(index, size):
        return [index] + [
            jnp.where(index + d >= size, index + d - size, index + d) for d in range(1, size)
        ]

    s_of = wrapped(s, NS) if NS <= 4 else None
    p_of, w_of = wrapped(p, NP), wrapped(w, NW)
    s_up = jnp.where(s + 1 >= NS, 0, s + 1)
    s_down = jnp.where(s == 0, NS - 1, s - 1)
    s_near = (s, s_up, s_down)
    p_near = (p, p_of[1], p_of[NP - 1])
    w_near = (w, w_of[1], w_of[NW - 1])

    def everyone(visit):
        def plane(ds, s_there):
            for dp in reversed(range(NP)):
                for dw in reversed(range(NW)):
                    if isinstance(ds, int) and (ds, dp, dw) == (0, 0, 0):
                        continue
                    visit((ds * NP + dp) * NW + dw - 1, (s_there, p_of[dp], w_of[dw]))

        if s_of is not None:
            for ds in reversed(range(1, NS)):
                plane(ds, s_of[ds])
        else:
            def step(ds, _):
                plane(ds, jnp.where(s + ds >= NS, s + ds - NS, s + ds))
                return 0

            lax.fori_loop(1, NS, step, 0)
        plane(0, s)

    barrier = pltpu.get_barrier_semaphore()

    loads = [
        pltpu.make_async_copy(source, target, loc_sem.at[n])
        for n, (source, target) in enumerate(
            (
                (spacing_hbm, spacing_ref), (conduct_hbm, conduct_ref), (temp_hbm, temp_ref),
                (cond_hbm, cond_ref), (diag_hbm, diag_ref), (map_hbm, map_ref),
                (vel_hbm, vel), (lhs_hbm, LHS),
            )
        )
    ]
    for load_ in loads:
        load_.start()
    everyone(
        lambda slot, there: pl.semaphore_signal(
            barrier, inc=1, device_id=there, device_id_type=MESH
        )
    )
    lane = lax.broadcasted_iota(jnp.int32, (1, lanes), 1)
    la = lane // (EY * EZ)
    lb = lane // EZ % EY
    lc = lane % EZ
    sub = lax.broadcasted_iota(jnp.int32, (8, lanes), 0)

    def column(values):
        result = jnp.full((8, lanes), float(values[0]), f32)
        for k in range(1, 8):
            result = jnp.where(sub == k, float(values[k]), result)
        return result

    def exists(ds, dw):
        conds = []
        if ds:
            conds.append((s + ds >= 0) & (s + ds < NS))
        if dw:
            conds.append((w + dw >= 0) & (w + dw < NW))
        if not conds:
            return None
        return conds[0] if len(conds) == 1 else conds[0] & conds[1]

    def under(cond, body):
        if cond is None:
            body()
        else:
            pl.when(cond)(body)

    for load_ in loads[:3]:
        load_.wait()
    sp0, sp1, sp2 = spacing_ref[0:1, :], spacing_ref[1:2, :], spacing_ref[2:3, :]
    conduct = conduct_ref[...]
    sx, sy, sz = 2.0 / sp0, 2.0 / sp1, 2.0 / sp2
    wk = column(WEIGHTS)
    mass_kn = wk * (sp0 * sp1 * sp2 / 8.0)
    for i in range(8):
        for j in range(8):
            m = float(WEIGHTS[i] * WEIGHTS[j]) * mass_kn
            MASS[i, j] = m
            T0[1, i, j] = m
            T0[0, i, j] = m * temp_ref[i, j]
    def view(field, ch, offset):
        return tuple([ch] + [slice(None) if d == 0 else side(d) for d in offset])

    axes = ((la, EX, EY * EZ), (lb, EY, EZ), (lc, EZ, 1))

    def local_assemble(field, channels):
        for ch in range(channels):
            for axis, (step, place, count) in enumerate(
                ((EY * EZ, la, EX), (EZ, lb, EY), (1, lc, EZ))
            ):
                lo = [ch, slice(None), slice(None), slice(None)]
                hi = list(lo)
                lo[axis + 1], hi[axis + 1] = 0, 7
                lo, hi = tuple(lo), tuple(hi)
                f0 = field[lo].reshape(64, lanes)
                f7 = field[hi].reshape(64, lanes)
                n7 = f7 + jnp.where(place < count - 1, roll(f0, -step, 1), 0.0)
                n0 = f0 + jnp.where(place > 0, roll(f7, step, 1), 0.0)
                field[lo] = n0.reshape(8, 8, lanes)
                field[hi] = n7.reshape(8, 8, lanes)

    def descriptor(rnd, send, recv, index):
        offset = OFFSETS[index]
        rows = pl.ds(START[offset], rows_of[offset])
        return pltpu.make_async_remote_copy(
            src_ref=send.at[:, rows, :],
            dst_ref=recv.at[:, rows, :],
            send_sem=face_ssem.at[rnd, index],
            recv_sem=face_rsem.at[rnd, index],
            device_id=(s_near[offset[0]], p_near[offset[1]], w_near[offset[2]]),
            device_id_type=MESH,
        )

    order = sorted(range(len(OFFSETS)), key=lambda i: -sum(1 for d in OFFSETS[i] if d))

    groups_to = {}
    for index in order:
        groups_to.setdefault((OFFSETS[index][0], OFFSETS[index][2]), []).append(index)

    def send_faces(rnd, field, channels, send, recv):
        for index in order:
            offset = OFFSETS[index]
            n_rows = rows_of[offset]
            free = sum(1 for d in offset if d == 0)
            for ch in range(channels):
                if free == 0:
                    i, j, k = [side(d) for d in offset]
                    value = jnp.broadcast_to(field[ch, i, j, k : k + 1, :], (8, lanes))
                elif free == 1:
                    value = field[view(field, ch, offset)]
                else:
                    face = field[view(field, ch, offset)].reshape(64, lanes)
                    axis = [n for n in range(3) if offset[n]][0]
                    place, count, step = axes[axis]
                    own = count - 1 if offset[axis] > 0 else 0
                    value = roll(face[0:n_rows], -own * step, 1)
                    for g in range(1, count):
                        piece = roll(face[g * n_rows : (g + 1) * n_rows], (g - own) * step, 1)
                        value = jnp.where(place == g, piece, value)
                send[ch, START[offset] : START[offset] + n_rows, :] = value
        if rnd == 0:
            pl.semaphore_wait(barrier, N - 1)
        for (ds, dw), indices in groups_to.items():
            def body(indices=indices):
                for index in indices:
                    descriptor(rnd, send, recv, index).start()

            under(exists(ds, dw), body)

    def take_faces(rnd, field, channels, send, recv):
        for (ds, dw), indices in groups_to.items():
            def body(indices=indices):
                for index in indices:
                    descriptor(rnd, send, recv, index).wait_recv()

            under(exists(-ds, -dw), body)
        for index in reversed(order):
            offset = OFFSETS[index]
            n_rows = rows_of[offset]
            free = sum(1 for d in offset if d == 0)
            back = tuple(-d for d in offset)
            shift = 0
            mask = None
            for d, (place, count, step) in zip(offset, axes):
                if d:
                    shift -= d * (count - 1) * step
                    here = place == (0 if d > 0 else count - 1)
                    mask = here if mask is None else mask & here
            there = exists(back[0], back[2])
            if there is not None:
                mask = mask & there
            start = START[offset]
            for ch in range(channels):
                value = recv[ch, start : start + n_rows, :]
                if free == 2:
                    axis = [n for n in range(3) if back[n]][0]
                    place, count, step = axes[axis]
                    own = count - 1 if back[axis] > 0 else 0
                    value = jnp.concatenate(
                        [roll(value, (own - g) * step, 1) for g in range(count)], axis=0
                    )
                else:
                    value = roll(value, shift, 1)
                value = jnp.where(mask, value, 0.0)
                if free == 0:
                    i, j, k = [side(d) for d in back]
                    field[ch, i, j, k : k + 1, :] = field[ch, i, j, k : k + 1, :] + value[0:1]
                else:
                    spot = view(field, ch, back)
                    old = field[spot]
                    field[spot] = old + value.reshape(old.shape)

    def drain_faces(rnd, send, recv):
        for index in order:
            offset = OFFSETS[index]

            def body(index=index):
                descriptor(rnd, send, recv, index).wait_send()

            under(exists(offset[0], offset[2]), body)

    groups = 64 // EZ
    s_dev = SX * SY
    half = groups // 2
    owners = 3 * SX
    reach = min(2, NS - 1)
    near = min(1, reach)
    edge = (w == 0) | (w == NW - 1)
    toward = jnp.where(w == 0, -1, 1)

    def split(value, size):
        if size & (size - 1):
            return value // size, value % size
        return lax.shift_right_logical(value, size.bit_length() - 1), value & (size - 1)

    local_assemble(T0, 2)
    for load_ in loads[3:6]:
        load_.wait()
    stat_send[0:SX] = cond_ref[...]
    stat_send[SX : 2 * SX] = diag_ref[...]

    codes = []
    for a in range(EX):
        t = map_ref[:, :, a, :].reshape(64, EY)
        owner, node = split(t, s_dev)
        row, col = split(node, SY)
        codes += [(owner * SX + row).astype(f32), col.astype(f32)]
    bi = lax.broadcasted_iota(jnp.int32, (EY, lanes), 0)
    spread = jnp.where(bi == lb, 1.0, 0.0).astype(jnp.bfloat16)
    spreads = jnp.dot(
        jnp.concatenate(codes, axis=0).astype(jnp.bfloat16), spread, preferred_element_type=f32
    )
    picked = []
    for part in range(2):
        full = spreads[part * 64 : (part + 1) * 64]
        for a in range(1, EX):
            full = jnp.where(
                la == a, spreads[(2 * a + part) * 64 : (2 * a + part + 1) * 64], full
            )
        packed = full[0:groups]
        for g in range(1, EZ):
            packed = jnp.where(lc == g, full[g * groups : (g + 1) * groups], packed)
        picked.append(packed)
    stat_send[2 * SX : 2 * SX + groups] = picked[0] * float(SY) + picked[1]

    area = jnp.where(lc == 0, conduct * sz * (sp0 * sp1 / 4.0), 0.0)
    for step in range(EZ.bit_length() - 1):
        area = area + roll(area, 1 << step, 1)
    area_send[...] = jnp.broadcast_to(area, (8, lanes))

    @pl.when(w == 0)
    def _():
        area_buf[near, 0] = area_send[...]


    qi = lax.broadcasted_iota(jnp.int32, (SY, lanes), 0)
    ri = lax.broadcasted_iota(jnp.int32, (owners, lanes), 0)
    others = [None] if NS == 2 else list(range(-1, 2, 2)) if NS > 2 else []

    def row_side(sign):
        return jnp.where(s == 0, 1, -1) if sign is None else sign

    def scatter_table(code, slot, rows, target):
        row, col = split(code.astype(jnp.int32), SY)
        row = row + (SX - SX * w)
        for g in range(groups):
            at = slice(g * lanes, (g + 1) * lanes)
            Bt[slot, :, at] = jnp.where(qi == col[g : g + 1], 1.0, 0.0).astype(jnp.bfloat16)
            target[:, at] = jnp.where(rows == row[g : g + 1], 1.0, 0.0)

    scatter_table(picked[0] * float(SY) + picked[1], 0, ri, Am)

    def receivers(visit, wanted):
        for ds in range(-reach, reach + 1):
            def body(ds=ds):
                for there in range(NW):
                    if there == 0:
                        plan = [(0, 0), (-1, 1), (1, -1), (-2, 2)]
                    elif there == NW - 1:
                        plan = [(0, 0), (1, 1), (-1, -1), (2, 2)]
                    else:
                        plan = [(0, 0), (-1, -1), (1, 1)]
                    for turn, (dp, place) in enumerate(plan):
                        full = dp == 0 or (place == 1 and there in (0, NW - 1))
                        if not wanted(full, ds) or (ds, dp, there) == (0, 0, 0):
                            continue
                        index = ((ds + reach) * NW + there) * 4 + turn
                        visit(full, ds, place, (s - ds, p_of[(-dp) % NP], there), index)

            under(exists(-ds, 0), body)

    def part_copy(ds, place, there=None, index=0):
        return pltpu.make_async_remote_copy(
            src_ref=part_send, dst_ref=part_buf.at[ds + reach, place],
            send_sem=part_ssem.at[index], recv_sem=part_rsem.at[ds + reach, place],
            device_id=(s, p, 0) if there is None else there, device_id_type=MESH,
        )

    def edge_copy(ds, place, there=None, index=0):
        return pltpu.make_async_remote_copy(
            src_ref=edge_send, dst_ref=edge_buf.at[ds + reach, place + 1],
            send_sem=part_ssem.at[index], recv_sem=edge_rsem.at[ds + reach, place + 1],
            device_id=(s, p, 0) if there is None else there, device_id_type=MESH,
        )

    def area_copy(ds, place, there=None, index=0):
        return pltpu.make_async_remote_copy(
            src_ref=area_send, dst_ref=area_buf.at[ds + near, place],
            send_sem=area_ssem.at[index], recv_sem=area_rsem.at[ds + near, place],
            device_id=(s, p, 0) if there is None else there, device_id_type=MESH,
        )

    def send_parts(what):
        def visit(full, ds, place, there, index):
            copy = (part_copy if full else edge_copy)(ds, place, there, index)
            copy.start() if what == "start" else copy.wait_send()

        receivers(visit, lambda full, ds: True)

    def send_areas(what):
        def visit(full, ds, place, there, index):
            copy = area_copy(ds, place, there, index)
            copy.start() if what == "start" else copy.wait_send()

        receivers(visit, lambda full, ds: full and abs(ds) <= near)

    def take(copy_of, ds, places):
        for place in places:
            copy_of(ds, place).wait_recv()

    def take_all(copy_of, bands, main, side, sides):
        for ds in bands:
            def body(ds=ds):
                if ds:
                    take(copy_of, ds, main)
                else:
                    pl.when(w != 0)(lambda: take(copy_of, ds, main))
                pl.when(edge)(lambda: take(copy_of, ds, side))
                if sides:
                    pl.when(jnp.logical_not(edge))(lambda: take(copy_of, ds, sides))

            under(exists(ds, 0), body)

    send_faces(0, T0, 2, send0, recv0)

    ring = NP * NW
    spot_c = p * NW + w
    ring_up = jnp.where(spot_c == ring - 1, 0, spot_c + 1)
    ring_down = jnp.where(spot_c == 0, ring - 1, spot_c - 1)
    q_at = {1: (ring_up // NW, ring_up % NW), 0: (p, w), -1: (ring_down // NW, ring_down % NW)}

    def patch_copy(index):
        dr, dc = AROUND[index]
        slot = (1 - dr) * 3 + (1 - dc)
        return pltpu.make_async_remote_copy(
            src_ref=stat_send,
            dst_ref=stat_buf.at[slot],
            send_sem=st_ssem.at[index],
            recv_sem=st_rsem.at[index],
            device_id=(s_near[dr],) + q_at[dc],
            device_id_type=MESH,
        )

    def patches(what):
        for index, (dr, dc) in enumerate(AROUND):
            def body(index=index):
                copy = patch_copy(index)
                if what == "start":
                    copy.start()
                elif what == "recv":
                    copy.wait_recv()
                else:
                    copy.wait_send()

            under(exists(-dr if what == "recv" else dr, 0), body)

    patches("start")
    pl.when(w == 0)(lambda: send_areas("start"))
    for slot in range(9):
        dr = slot // 3 - 1
        if dr:
            @pl.when(jnp.logical_not(exists(dr, 0)))
            def _(slot=slot):
                stat_buf[slot] = jnp.ones(stat_send.shape, f32)
    stat_buf[4] = stat_send[...]

    keep_lane = jnp.where((lc == 0) & (w == 0), 0.0, 1.0)
    keep = jnp.where(sub == 0, jnp.broadcast_to(keep_lane, (8, lanes)), 1.0)

    take_faces(0, T0, 2, send0, recv0)
    for i in range(8):
        inv = keep / T0[1, i]
        T[0, i] = T0[0, i] * inv
        INVA[i] = inv * TIME_STEP
    for load_ in loads[6:]:
        load_.wait()

    cxx, cyy, czz = conduct * sx, conduct * sy, conduct * sz

    def side_table(code, slot):
        code = code.astype(jnp.int32)
        node = lax.broadcasted_iota(jnp.int32, (2 * SX, lanes), 0)
        first = jnp.where(w == 0, (NW - 1) * s_dev + SY - 2, 0)
        node = first + node % SX * SY + node // SX
        for g in range(groups):
            Side[slot, :, g * lanes : (g + 1) * lanes] = jnp.where(
                node == code[g : g + 1], 1.0, 0.0
            ).astype(jnp.bfloat16)

    def other_tables():
        patches("recv")
        side_table(stat_buf[4 + toward, 2 * SX : 2 * SX + groups], 0)
        for n, sign in enumerate(others):
            sign = row_side(sign)
            slot = (sign + 1) * 3 + 1
            ro = lax.broadcasted_iota(jnp.int32, (8, lanes), 0)
            rows = ro // 2 * SX + ro % 2 + jnp.where(sign > 0, 0, SX - 2)
            scatter_table(
                stat_buf[slot, 2 * SX : 2 * SX + groups], n + 1, rows, Am_other.at[n]
            )
            side_table(stat_buf[slot + toward, 2 * SX : 2 * SX + groups], n + 1)

    def fold(values):
        for width in (4, 2, 1):
            low = sub // width % 2 == 0
            count = len(values) // 2
            values = [
                jnp.where(low, values[n], values[n + count])
                + jnp.where(
                    low,
                    roll(values[n], -width, 0),
                    roll(values[n + count], width, 0),
                )
                for n in range(count)
            ]
        return values[0]

    normal_row = column(MATRIX[0])

    def wall_part():
        across_row = [normal_row] * 8
        across_row[0] = jnp.where(lb == 0, 0.5 * normal_row, normal_row)
        across_row[7] = jnp.where(lb == EY - 1, 0.5 * normal_row, normal_row)
        rows = []
        for i in range(8):
            scale = None
            if i == 0:
                scale = jnp.where((la == 0) & (s > 0), 0.5, 1.0)
            elif i == 7:
                scale = jnp.where((la == EX - 1) & (s < NS - 1), 0.5, 1.0)
            terms = []
            for j in range(8):
                weight = across_row[j] if scale is None else across_row[j] * scale
                terms.append(T[0, i, j] * weight + R[0, i, j] * (INVA[i, j] * normal_row))
            rows.append(jnp.where(lc == 0, fold(terms), 0.0))
        flat = jnp.concatenate(rows, axis=0)
        packed = flat[0:groups]
        for g in range(1, EZ):
            packed = packed + roll(flat[g * groups : (g + 1) * groups], g, 1)
        part_send[...] = packed
        edge_send[...] = jnp.where(
            (sub == 0) | (sub == 7), packed[0:half], roll(packed[half:groups], 2, 0)
        )
        part_buf[reach, 0] = packed
        send_parts("start")

    for rnd in range(1, SUBSTEPS + 1):
        send, recv = (send1, recv1) if rnd == 1 else (send2, recv2)
        def terms(get, top, bottom):
            value = jnp.concatenate(
                [jnp.concatenate([get(4 * h + q) for q in range(4)], axis=0) for h in range(2)],
                axis=1,
            )
            high = value.astype(jnp.bfloat16)
            low = (value - high.astype(f32)).astype(jnp.bfloat16)
            rhs = jnp.concatenate([high, low, high], axis=0)
            return jnp.dot(LHS[top:bottom, :], rhs, preferred_element_type=f32)

        def piece(found, kind, at):
            rows = kind * 256 + (at % 4) * 64
            cols = (at // 4) * lanes
            return found[rows : rows + 64, cols : cols + lanes].reshape(8, 8, lanes)

        along = terms(lambda j: T[0, :, j].reshape(64, lanes), 0, 512)
        for j in range(8):
            grad, stiff = piece(along, 0, j), piece(along, 1, j)
            R[0, :, j] = sx * (vel[0, :, j].astype(f32) * grad + cxx * stiff)
        across = terms(lambda i: T[0, i].reshape(64, lanes), 0, 1024)
        for i in range(8):
            total = R[0, i]
            total = total + sy * (
                vel[1, i].astype(f32) * piece(across, 0, i) + cyy * piece(across, 1, i)
            )
            total = total + sz * (
                vel[2, i].astype(f32) * piece(across, 2, i) + czz * piece(across, 3, i)
            )
            R[0, i] = -(MASS[i] * total)
        local_assemble(R, 1)
        if rnd == SUBSTEPS:
            pl.when(w == 0)(lambda: wall_part())
        send_faces(rnd, R, 1, send, recv)
        if rnd < SUBSTEPS:
            if rnd == 1:
                other_tables()
            take_faces(rnd, R, 1, send, recv)
            for a in range(8):
                T[0, a] = keep * T[0, a] + R[0, a] * INVA[a]

    def wide(get):
        return jnp.concatenate(
            [jnp.concatenate([get(3 * r + c) for c in range(3)], axis=1) for r in range(3)], axis=0
        )

    cond = wide(lambda slot: stat_buf[slot, 0:SX])
    diag = wide(lambda slot: stat_buf[slot, SX : 2 * SX])
    grow = s * SX - SX + lax.broadcasted_iota(jnp.int32, cond.shape, 0)
    cup = jnp.where(grow != NS * SX - 1, 0.5 * (cond + roll(cond, -1, 0)), 0.0)
    cdown = jnp.where(grow != 0, 0.5 * (cond + roll(cond, 1, 0)), 0.0)
    cright = 0.5 * (cond + roll(cond, -1, 1))
    cleft = 0.5 * (cond + roll(cond, 1, 1))
    jacobi = diag + cup + cdown + cright + cleft
    inv_jacobi = 1.0 / jacobi

    def apply(v):
        return (
            jacobi * v
            - cup * roll(v, -1, 0)
            - cdown * roll(v, 1, 0)
            - cright * roll(v, -1, 1)
            - cleft * roll(v, 1, 1)
        )

    def centre(v):
        return v[SX : 2 * SX, SY : 2 * SY]

    point = lax.broadcasted_iota(jnp.int32, (groups, lanes), 0) + lc * groups
    wi = jnp.full((groups, lanes), float(WEIGHTS[0]), f32)
    wj = jnp.full((groups, lanes), float(WEIGHTS[0]), f32)
    for k in range(1, 8):
        wi = jnp.where(point // 8 == k, float(WEIGHTS[k]), wi)
        wj = jnp.where(point % 8 == k, float(WEIGHTS[k]), wj)
    wij = wi * wj

    take_all(area_copy, range(-near, near + 1), (0,), (1,), ())
    bands = range(-reach, reach + 1)
    take_all(part_copy, bands, (0,), (1,), ())
    take_all(edge_copy, bands, (), (-1, 2), (-1, 1))

    def both(mask, cond):
        return mask if cond is None else mask & cond

    def edge_rows(part):
        return jnp.where(
            (sub == 0) | (sub == 7), part[0:half], roll(part[half:groups], 2, 0)
        )

    def span_sum(part, above, below):
        above = roll(above, (EY - 1) * EZ, 1)
        below = roll(below, -(EY - 1) * EZ, 1)
        high = (sub == 7) & (lb == EY - 1)
        low = (sub == 0) & (lb == 0)
        rows = []
        for h, (first, last) in enumerate(((0, 7), (2, 1))):
            rows.append(
                part[h * half : (h + 1) * half]
                + jnp.where(high, above[first : first + 1], 0.0)
                + jnp.where(low, below[last : last + 1], 0.0)
            )
        return rows

    def band_sum(ds):
        mains, sides = part_buf[ds + reach, 0], part_buf[ds + reach, 1]
        back, ahead, far = [edge_buf[ds + reach, place + 1] for place in (-1, 1, 2)]
        main_edge = edge_rows(mains)
        ahead = jnp.where(edge, edge_rows(sides), ahead)
        up = toward > 0
        return (
            span_sum(mains, jnp.where(up, ahead, back), jnp.where(up, back, ahead)),
            span_sum(sides, jnp.where(up, far, main_edge), jnp.where(up, main_edge, far)),
        )

    jump = (EX - 1) * EY * EZ + EZ - 1
    last = (la == EX - 1) & (lc == EZ - 1)
    first = (la == 0) & (lc == 0)

    def stream_sum(here, above, below):
        even, odd = here
        if above is not None:
            odd = odd + jnp.where(both(last, above[1]), roll(above[0][0], jump, 1), 0.0)
        if below is not None:
            even = even + jnp.where(both(first, below[1]), roll(below[0][1], -jump, 1), 0.0)
        return even, odd

    def halves(pair, scale, valid):
        flux = jnp.concatenate([pair[0] * scale, pair[1] * scale], axis=0) * wij
        if valid is not None:
            flux = jnp.where(valid, flux, 0.0)
        high = flux.astype(jnp.bfloat16).astype(f32)
        return high, flux - high

    def spread_rows(v, count):
        return jnp.concatenate(
            [jnp.broadcast_to(v[g : g + 1], (count, lanes)) for g in range(groups)], axis=1
        )

    def contract(left, right):
        return lax.dot_general(
            left, right, (((1,), (1,)), ((), ())), preferred_element_type=f32
        )

    def main_load(parts, table, slot, count):
        left = jnp.concatenate([table * spread_rows(v, count) for v in parts], axis=0)
        out = contract(left.astype(jnp.bfloat16), Bt[slot])
        return out[0:count] + out[count : 2 * count]

    column_at = lax.broadcasted_iota(jnp.int32, (SX, SY), 1) - jnp.where(w == 0, SY - 2, 0)

    def side_load(parts, slot):
        right = jnp.concatenate([spread_rows(v, 8) for v in parts], axis=0)
        out = contract(Side[slot], right.astype(jnp.bfloat16))
        out = out[:, 0:1] + out[:, 8:9]
        return jnp.where(
            column_at == 0, out[0:SX], jnp.where(column_at == 1, out[SX : 2 * SX], 0.0)
        )

    def block(columns, side):
        columns[0] = columns[0] + jnp.where(w == 0, side, 0.0)
        columns[2] = columns[2] + jnp.where(w == NW - 1, side, 0.0)
        return jnp.concatenate(columns, axis=1)

    none = jnp.zeros((SX, 3 * SY), f32)
    if NS == 2:
        sign = row_side(None)
        own, other = band_sum(0), band_sum(sign)
        ahead, behind = exists(1, 0), exists(-1, 0)
        bands_summed = [
            [
                stream_sum(own[kind], (other[kind], ahead), (other[kind], behind))
                for kind in range(2)
            ],
            [
                stream_sum(other[kind], (own[kind], behind), (own[kind], ahead))
                for kind in range(2)
            ],
        ]
        offsets = [0, sign]
    else:
        found_at = {ds: band_sum(ds) for ds in bands}
        bands_summed, offsets = [], [0] + others
        for ds in offsets:
            bands_summed.append(
                [
                    stream_sum(
                        found_at[ds][kind],
                        (found_at[ds + 1][kind], exists(ds + 1, 0)) if ds < reach else None,
                        (found_at[ds - 1][kind], exists(ds - 1, 0)) if ds > -reach else None,
                    )
                    for kind in range(2)
                ]
            )
    top, bottom = none, none
    for n, ds in enumerate(offsets):
        here = None if n == 0 or NS == 2 else exists(ds, 0)
        areas = [area_buf[ds + near, kind] for kind in range(2)]
        beside = side_load(
            halves(bands_summed[n][1], areas[1], edge if here is None else edge & here), n
        )
        main = halves(bands_summed[n][0], areas[0], here)
        if n == 0:
            found = main_load(main, Am[...], 0, owners)
            middle = block([found[c * SX : (c + 1) * SX] for c in range(3)], beside)
            continue
        found = main_load(main, Am_other[n - 1], n, 8)
        if NS == 2 or ds > 0:
            rows = block([jnp.where(sub < 2, roll(found, -2 * c, 0), 0.0) for c in range(3)], beside)
            bottom = jnp.where(ahead, rows, 0.0) if NS == 2 else rows
        if NS == 2 or ds < 0:
            rows = block(
                [jnp.where(sub > 5, roll(found, 6 - 2 * c, 0), 0.0) for c in range(3)], beside
            )
            top = jnp.where(behind, rows, 0.0) if NS == 2 else rows
    load_wide = jnp.concatenate([top, middle, bottom], axis=0)
    load = centre(load_wide)
    z_wide = load_wide * inv_jacobi
    z_mine = centre(z_wide)
    image_wide = apply(z_wide)
    y_wide = image_wide * inv_jacobi
    ay = centre(apply(y_wide))
    image = centre(image_wide)
    y = centre(y_wide)

    def rowsum(v):
        return jnp.sum(v, axis=0, keepdims=True)

    fourth = SY // 4
    line = lax.broadcasted_iota(jnp.int32, (1, SY), 1) // fourth

    def folded(v):
        v = rowsum(v)
        v = v + roll(v, SY // 2, 1)
        return v + roll(v, SY // 4, 1)

    mine = folded(load * z_mine)
    for place, product in enumerate((z_mine * image, image * y, y * ay)):
        mine = jnp.where(line == place + 1, folded(product), mine)
    sum_send[...] = mine
    sum_buf[N - 1 : N, :] = mine

    def sum_copy(slot, there):
        return pltpu.make_async_remote_copy(
            src_ref=sum_send,
            dst_ref=sum_buf.at[pl.ds(slot, 1), :],
            send_sem=p_ssem.at[0],
            recv_sem=p_rsem.at[0],
            device_id=there,
            device_id_type=MESH,
        )

    everyone(lambda slot, there: sum_copy(slot, there).start())

    take_faces(SUBSTEPS, R, 1, send2, recv2)
    for a in range(8):
        out_temp[a] = keep * T[0, a] + R[0, a] * INVA[a]

    for rnd, (send, recv) in enumerate(((send0, recv0), (send1, recv1), (send2, recv2))):
        drain_faces(rnd, send, recv)
    patches("send")

    @pl.when(w == 0)
    def _():
        send_areas("send")
        send_parts("send")

    arrived = sum_buf.at[pl.ds(0, N - 1), :]
    pltpu.make_async_copy(arrived, arrived, p_ssem.at[0]).wait()
    pltpu.make_async_copy(arrived, arrived, p_rsem.at[0]).wait()
    totals = jnp.sum(sum_buf[...], axis=0, keepdims=True)
    rz, curve, m, q = [
        jnp.sum(jnp.where(line == place, totals, 0.0), axis=1, keepdims=True) for place in range(4)
    ]
    alpha = rz / curve
    new = alpha * alpha * m - rz
    beta = new / rz
    one = 1.0 + beta
    curve_next = one * one * curve - 2.0 * one * alpha * m + alpha * alpha * q
    alpha_next = new / curve_next
    direction = one * z_mine - alpha * y
    out_shell[...] = alpha * z_mine + alpha_next * direction
    out_resid[...] = load - alpha * image - alpha_next * (one * image - alpha * ay)


def hand_over(a_ref, b_ref, c_ref, x_ref, y_ref, z_ref):
    x_ref[...] = a_ref[...]
    y_ref[...] = b_ref[...]
    z_ref[...] = c_ref[...]


def per_device(sizes, temp_in, velocity, spacing, conduct, shell_map, shell_cond, shell_diag):
    NS, NP, NW = sizes
    N = NS * NP * NW
    lanes = temp_in.shape[3]
    EX, EY = shell_map.shape[2:]
    EZ = lanes // (EX * EY)
    groups = 64 // EZ
    reach = min(2, NS - 1)
    near = min(1, reach)
    others = min(NS - 1, 2)
    SX, SY = shell_cond.shape
    assert lanes == SY and SX == 8 and groups == 16 and NP > 2 and NW > 1
    ROWS = face_layout((EX, EY, EZ))[2]
    lhs = jnp.asarray(mxu_tables())
    f32 = jnp.float32
    block = (8, 8, 8, lanes)
    vmem = pl.BlockSpec(memory_space=pltpu.VMEM)
    V = pltpu.VMEM
    dma = pltpu.SemaphoreType.DMA
    outs = pl.pallas_call(
        functools.partial(kernel, (NS, NP, NW, EX, EY, EZ)),
        out_shape=(
            pltpu.VMEM(block, f32),
            pltpu.VMEM((SX, SY), f32),
            pltpu.VMEM((SX, SY), f32),
        ),
        in_specs=[pl.BlockSpec(memory_space=pltpu.HBM)] * 8,
        out_specs=(vmem, vmem, vmem),
        scratch_shapes=[
            V(block, f32), V((3,) + block, jnp.bfloat16), V(lhs.shape, jnp.bfloat16),
            V((3, lanes), f32), V((1, lanes), f32), V(shell_map.shape, jnp.int32),
            V((SX, SY), f32), V((SX, SY), f32),
            V((2,) + block, f32), V((1,) + block, f32), V((1,) + block, f32),
            V(block, f32), V(block, f32),
            V((2, ROWS, lanes), f32), V((2, ROWS, lanes), f32),
            V((1, ROWS, lanes), f32), V((1, ROWS, lanes), f32),
            V((1, ROWS, lanes), f32), V((1, ROWS, lanes), f32),
            V((groups, lanes), f32), V((8, lanes), f32), V((8, lanes), f32),
            V((2 * reach + 1, 2, groups, lanes), f32), V((2 * reach + 1, 4, 8, lanes), f32),
            V((2 * near + 1, 2, 8, lanes), f32),
            V((others + 1, SY, groups * lanes), jnp.bfloat16),
            V((3 * SX, groups * lanes), f32), V((max(others, 1), 8, groups * lanes), f32),
            V((others + 1, 2 * SX, groups * lanes), jnp.bfloat16),
            V((2 * SX + groups, SY), f32), V((9, 2 * SX + groups, SY), f32),
            V((1, SY), f32), V((N, SY), f32),
            dma((3, len(OFFSETS))), dma((3, len(OFFSETS))),
            dma(((2 * reach + 1) * NW * 4,)), dma((2 * reach + 1, 2)), dma((2 * reach + 1, 4)),
            dma(((2 * reach + 1) * NW * 4,)), dma((2 * near + 1, 2)),
            dma((8,)), dma((8,)), dma((1,)), dma((1,)), dma((8,)),
        ],
        compiler_params=pltpu.CompilerParams(
            collective_id=0, has_side_effects=True, vmem_limit_bytes=24 << 20
        ),
    )(
        *[
            pltpu.with_memory_space_constraint(x, pltpu.HBM)
            for x in (
                temp_in, velocity, lhs, spacing, conduct.reshape(1, lanes), shell_map, shell_cond,
                shell_diag,
            )
        ]
    )
    return pl.pallas_call(
        hand_over,
        out_shape=tuple(jax.ShapeDtypeStruct(o.shape, o.dtype) for o in outs),
        in_specs=[vmem] * 3,
        out_specs=(vmem,) * 3,
        compiler_params=pltpu.CompilerParams(vmem_limit_bytes=4 << 20),
    )(*outs)


def solution(mesh):
    sizes = (mesh.shape["stream"], mesh.shape["span"], mesh.shape["wall"])
    return jax.shard_map(
        functools.partial(per_device, sizes),
        mesh=mesh,
        in_specs=(
            P(None, None, None, ("stream", "span", "wall")),
            P(None, None, None, None, ("stream", "span", "wall")),
            P(None, ("stream", "span", "wall")),
            P(("stream", "span", "wall")),
            P(None, None, "stream", "span"),
            P("stream", ("span", "wall")),
            P("stream", ("span", "wall")),
        ),
        out_specs=(
            P(None, None, None, ("stream", "span", "wall")),
            P("stream", ("span", "wall")),
            P("stream", ("span", "wall")),
        ),
        check_vma=False,
    )
```
